32 devices in a mesh: member: 2 (over core), tp: 16 (over z, y, x).
Axes of the slice: x: 2, y: 2, z: 4, core: 2. Of those that a mesh axis runs over, the one named last changes fastest.
Arguments:
- stream_in: bfloat16 [512, 4096], P(('member', 'tp')), may hold values from -6 to 6
- kv_cache: bfloat16 [512, 512, 2048], P(('member', 'tp')), may hold values from -400 to 400
- lengths: int32 [128], replicated, may hold values from 1 to 512
- targets: int32 [128], replicated, may hold values from 0 to 65535
- norm_gains: float32 [3, 4096], replicated, may hold values from 0.1 to 1.9
- w_qkv: bfloat16 [4096, 6144], P(None, 'tp'), may hold values from -0.09375 to 0.09375
- w_out: bfloat16 [4096, 4096], P('tp'), may hold values from -0.09375 to 0.09375
- w_gate_up: bfloat16 [2, 4096, 14336], P(None, None, 'tp'), may hold values from -0.09375 to 0.09375
- w_down: bfloat16 [14336, 4096], P('tp'), may hold values from -0.046875 to 0.046875
- lm_head: bfloat16 [4096, 65536], P(None, 'tp'), may hold values from -300 to 300
- fast_in: float32 [4, 2, 4096], P('member'), may hold values from 0.1 to 1.9
- fast_hidden: float32 [4, 3, 14336], P('member', None, 'tp'), may hold values from 0.1 to 1.9
- fast_out: float32 [4, 4096], P('member'), may hold values from 0.1 to 1.9
Outputs:
- mean_logits: bfloat16 [128, 65536], P(None, 'tp')
- token_logprob: float32 [128], replicated
The draws below stay inside these ranges and needn't reach their ends.
Inputs may be any that keep to these rules, and one draw needn't show every extreme that they name: lengths is the same for all members.
All inputs are finite; a program needn't handle non-finite values.
Results may differ from the reference program's by a relative error of at most 0.02.
Values may be sent and summed in bfloat16 or wider, within the bound.
No kernel may reach another device: no remote copies, remote signals or barrier semaphores. Data moves between devices by JAX's collectives and lax.ppermute only.
A program may use at most 192 MiB of HBM per device.

```python
import math
import jax
import jax.numpy as jnp
import numpy as np
from jax import lax

D = 4096
HEADS = 32
KV = 8
HD = 128
FF = 14336
VOCAB = 65536
B = 128
CACHE = 512
MEMBERS = 4


def draw_kv_cache(key, part):
    row_total = MEMBERS * B
    array_shape = (row_total, CACHE, 2 * KV * HD)
    key_main = jax.random.fold_in(key, 11)
    raw_draw = jnp.clip(jax.random.normal(key_main, array_shape, jnp.float32), -6.0, 6.0)
    return raw_draw.astype(jnp.bfloat16)


def draw_lm_head(key, part):
    array_shape = (D, VOCAB)
    key_main = jax.random.fold_in(key, 61)
    spread_scale = 3.0 / math.sqrt(D)
    result = jnp.clip(jax.random.normal(key_main, array_shape, jnp.float32) * spread_scale, -6.0 * spread_scale, 6.0 * spread_scale)
    return result.astype(jnp.bfloat16)


def with_ends(values, stream_key, low, largest):
    longest = values.shape.index(max(values.shape))
    spots = []
    for shift in (0, 1):
        where = [jax.random.randint(jax.random.fold_in(stream_key, axis), (), 0, length) for axis, length in enumerate(values.shape)]
        where[longest] = (where[longest] + shift) % values.shape[longest]
        spots.append(tuple(where))
    return values.at[spots[0]].set(low).at[spots[1]].set(largest)


def shard_levels(own_key, shape, shards, least, high):
    def one(axis_at, blocks):
        steps = jax.random.uniform(jax.random.fold_in(jax.random.fold_in(own_key, 6), axis_at), (blocks,), jnp.float32, least / len(shards), high / len(shards))
        return jnp.repeat(jnp.exp(steps), shape[axis_at] // blocks).reshape((-1,) + (1,) * (len(shape) - axis_at - 1))

    factor_of = one(*shards[0])
    for cut in shards[1:]:
        factor_of = factor_of * one(*cut)
    return factor_of


def rank_bounds(amount, skew):
    portions = [(1 << 20) // math.isqrt(grade ** skew) + 1 for grade in range(1, amount + 1)]
    deviation = 1 + sum(portions) // (1 << 30)
    return np.cumsum(np.array([max(1, weight // deviation) for weight in portions]))


def skewed_ids(stream_key, shape, number_of, slope):
    grid = rank_bounds(number_of, slope)
    lot = jax.random.randint(jax.random.fold_in(stream_key, 1), shape, 0, int(grid[number_of - 1]))
    grade = jnp.searchsorted(jnp.asarray(grid, jnp.int32), lot, side="right")
    return jax.random.permutation(jax.random.fold_in(stream_key, 2), number_of)[grade].astype(jnp.int32)


def noise(rng, shape, scale, most, cuts=(), held_as=jnp.bfloat16):
    values = scale * jax.random.normal(rng, shape, jnp.float32)
    if cuts:
        values = values * shard_levels(rng, shape, cuts, -0.22, 0.18)
    return jnp.clip(values, -most, most).astype(held_as)


def setup_inputs(seed: int = 0) -> dict:
    keys = jax.random.split(jax.random.key(seed), 14)
    return {
        "stream_in": noise(keys[0], (MEMBERS * B, D), 1.0, 6.0, ((0, 32),)),
        "kv_cache": draw_kv_cache(jax.random.fold_in(keys[13], 71), 0),
        "lengths": with_ends(jax.random.randint(keys[2], (B,), 1, CACHE + 1), jax.random.fold_in(keys[2], 1), 1, CACHE).astype(jnp.int32),
        "targets": with_ends(skewed_ids(keys[3], (B,), VOCAB, 2), jax.random.fold_in(keys[3], 3), 0, VOCAB - 1).astype(jnp.int32),
        "norm_gains": jnp.clip(1.0 + 0.18 * jax.random.normal(keys[4], (3, D), jnp.float32), 0.1, 1.9),
        "w_qkv": noise(keys[5], (D, (HEADS + 2 * KV) * HD), D ** -0.5, 0.09375, ((1, 16),)),
        "w_out": noise(keys[6], (HEADS * HD, D), (HEADS * HD) ** -0.5, 0.09375, ((0, 16),)),
        "w_gate_up": noise(keys[7], (2, D, FF), D ** -0.5, 0.09375, ((2, 16),)),
        "w_down": noise(keys[8], (FF, D), FF ** -0.5, 0.046875, ((0, 16),)),
        "lm_head": draw_lm_head(jax.random.fold_in(keys[13], 71), 0),
        "fast_in": jnp.clip(1.0 + 0.18 * jax.random.normal(keys[10], (MEMBERS, 2, D), jnp.float32), 0.1, 1.9),
        "fast_hidden": jnp.clip(1.0 + 0.18 * jax.random.normal(keys[11], (MEMBERS, 3, FF), jnp.float32), 0.1, 1.9),
        "fast_out": jnp.clip(1.0 + 0.18 * jax.random.normal(keys[12], (MEMBERS, D), jnp.float32), 0.1, 1.9),
    }


ROPE_BASE = 500000.0

def rms_norm(values_in, gain):
    return values_in * lax.rsqrt(lax.optimization_barrier(jnp.mean(values_in * values_in, axis=-1, keepdims=True)) + 1e-05) * gain

def rotate(values_in, positions):
    half_dim = values_in.shape[-1] // 2
    frequency = ROPE_BASE ** (-jnp.arange(half_dim, dtype=jnp.float32) * 2.0 / values_in.shape[-1])
    angles = positions.astype(jnp.float32)[:, None, None] * frequency[None, None, :]
    lower_half = values_in[..., :half_dim]
    upper_half = values_in[..., half_dim:]
    return jnp.concatenate([lower_half * jnp.cos(angles) - upper_half * jnp.sin(angles), upper_half * jnp.cos(angles) + lower_half * jnp.sin(angles)], axis=-1)

def attend(projected, cache_rows, positions):
    row_count = projected.shape[0]
    head_cols = HEADS * HD
    kv_cols = KV * HD
    queries = rotate(projected[:, :head_cols].astype(jnp.float32).reshape(row_count, HEADS, HD), positions).astype(jnp.bfloat16)
    new_key = rotate(projected[:, head_cols:head_cols + kv_cols].astype(jnp.float32).reshape(row_count, KV, HD), positions).astype(jnp.bfloat16)
    new_value = projected[:, head_cols + kv_cols:].reshape(row_count, KV, HD)
    cache_keys = cache_rows[:, :, :kv_cols].reshape(row_count, CACHE, KV, HD)
    cache_values = cache_rows[:, :, kv_cols:].reshape(row_count, CACHE, KV, HD)
    grouped = queries.reshape(row_count, KV, HEADS // KV, HD).astype(jnp.float32)
    inv_root = HD ** (-0.5)
    cached = jnp.einsum('rkgd,rckd->rkgc', grouped, cache_keys.astype(jnp.float32)) * inv_root
    fresh = jnp.einsum('rkgd,rkd->rkg', grouped, new_key.astype(jnp.float32)) * inv_root
    in_cache = jnp.arange(CACHE)[None, :] < positions[:, None]
    cached = jnp.where(in_cache[:, None, None, :], cached, -1e+30)
    peak = jnp.maximum(lax.optimization_barrier(jnp.max(cached, axis=-1)), fresh)
    weights = jnp.exp(cached - peak[..., None])
    fresh_w = jnp.exp(fresh - peak)
    total_sum = lax.optimization_barrier(jnp.sum(weights, axis=-1)) + fresh_w
    probs = (weights / total_sum[..., None]).astype(jnp.bfloat16)
    fresh_p = (fresh_w / total_sum).astype(jnp.bfloat16)
    result = jnp.einsum('rkgc,rckd->rkgd', probs.astype(jnp.float32), cache_values.astype(jnp.float32))
    result = result + fresh_p.astype(jnp.float32)[..., None] * new_value.astype(jnp.float32)[:, :, None, :]
    return result.reshape(row_count, HEADS * HD).astype(jnp.bfloat16)

def reference(stream_in, kv_cache, lengths, targets, norm_gains, w_qkv, w_out, w_gate_up, w_down, lm_head, fast_in, fast_hidden, fast_out):
    row_count = stream_in.shape[0]
    positions = jnp.tile(lengths, MEMBERS).astype(jnp.int32)
    attn_in = rms_norm(stream_in.astype(jnp.float32), norm_gains[0]).astype(jnp.bfloat16)
    projected = jnp.dot(attn_in, w_qkv, preferred_element_type=jnp.float32).astype(jnp.bfloat16)
    blocks = lax.map(lambda block_item: attend(block_item[0], block_item[1], block_item[2]), (projected.reshape(row_count // 8, 8, -1), kv_cache.reshape(row_count // 8, 8, CACHE, 2 * KV * HD), positions.reshape(row_count // 8, 8)))
    attended = blocks.reshape(row_count, HEADS * HD)
    middle = (stream_in.astype(jnp.float32) + jnp.dot(attended, w_out, preferred_element_type=jnp.float32)).astype(jnp.bfloat16)
    ffn_in = rms_norm(middle.astype(jnp.float32), norm_gains[1]).astype(jnp.bfloat16)
    grouped = ffn_in.astype(jnp.float32).reshape(MEMBERS, B, D)
    gate_in = (grouped * fast_in[:, 0][:, None, :]).astype(jnp.bfloat16).reshape(row_count, D)
    up_in = (grouped * fast_in[:, 1][:, None, :]).astype(jnp.bfloat16).reshape(row_count, D)
    gate_act = jnp.dot(gate_in, w_gate_up[0], preferred_element_type=jnp.float32).reshape(MEMBERS, B, FF) * fast_hidden[:, 0][:, None, :]
    up_act = jnp.dot(up_in, w_gate_up[1], preferred_element_type=jnp.float32).reshape(MEMBERS, B, FF) * fast_hidden[:, 1][:, None, :]
    hidden = (jax.nn.silu(gate_act) * up_act * fast_hidden[:, 2][:, None, :]).astype(jnp.bfloat16).reshape(row_count, FF)
    down_sum = jnp.dot(hidden, w_down, preferred_element_type=jnp.float32).reshape(MEMBERS, B, D) * fast_out[:, None, :]
    layer_out = (middle.astype(jnp.float32).reshape(MEMBERS, B, D) + down_sum).astype(jnp.bfloat16).reshape(row_count, D)
    final_in = rms_norm(layer_out.astype(jnp.float32), norm_gains[2]).astype(jnp.bfloat16)
    logits = jnp.dot(final_in, lm_head, preferred_element_type=jnp.float32)
    mean_logit = lax.optimization_barrier(jnp.sum(logits.reshape(MEMBERS, B, VOCAB), axis=0)) / MEMBERS
    peak = lax.optimization_barrier(jnp.max(mean_logit, axis=-1))
    log_total = peak + jnp.log(lax.optimization_barrier(jnp.sum(jnp.exp(mean_logit - peak[:, None]), axis=-1)))
    target_logit = lax.optimization_barrier(jnp.sum(jnp.where(jnp.arange(VOCAB)[None, :] == targets[:, None], mean_logit, 0.0), axis=-1))
    return (mean_logit.astype(jnp.bfloat16), target_logit - log_total)
```

```python
import jax
import jax.numpy as jnp
from jax import lax
from jax.experimental import pallas as pl
from jax.experimental.pallas import tpu as pltpu
from jax.sharding import PartitionSpec as P

HEADS = 32
KV = 8
HD = 128


ROPE_BASE = 500000.0


def rms_norm(values_in, gain):
    return (
        values_in
        * lax.rsqrt(jnp.mean(values_in * values_in, axis=-1, keepdims=True) + 1e-05)
        * gain
    )


def swap_with(values, tp_count, mask):
    return lax.ppermute(values, "tp", [(i, i ^ mask) for i in range(tp_count)])


def far_digits(tp_count):
    digits, stride = [], 4
    while stride < tp_count:
        size = min(4, tp_count // stride)
        digits.append((stride, size))
        stride *= size
    return digits


def gather_far(block, tp_count):
    values = block[None]
    for stride, size in far_digits(tp_count):
        parts = [values] + [swap_with(values, tp_count, stride * j) for j in range(1, size)]
        values = jnp.concatenate(parts, axis=0)
    return values


def gather_near(values, tp_count):
    half = values.shape[-1] // 2
    left, right = values[..., :half], values[..., half:]
    left = jnp.stack([left, swap_with(left, tp_count, 2)], axis=1)
    right = jnp.stack([right, swap_with(right, tp_count, 1)], axis=1)
    left = jnp.stack([left, swap_with(left, tp_count, 1)], axis=2)
    right = jnp.stack([right, swap_with(right, tp_count, 2)], axis=2)
    right = jnp.swapaxes(right, 1, 2)
    return jnp.concatenate([left, right], axis=-1)


def gather_rows(block, tp_count):
    rows, width = block.shape
    return gather_near(gather_far(block, tp_count), tp_count).reshape(tp_count * rows, width)


def scatter_rows(partial, tp_count):
    wide, narrow = jnp.float32, jnp.bfloat16
    rows = partial.shape[0] // tp_count
    width = partial.shape[1]
    half = width // 2
    blocks = partial.reshape(tp_count // 4, 2, 2, rows, width)

    def add(kept, sent, mask):
        return kept + swap_with(sent.astype(narrow), tp_count, mask).astype(wide)

    left, right = blocks[..., :half], blocks[..., half:]
    left = add(left[:, :, 0], left[:, :, 1], 1)
    right = add(right[:, 0], right[:, 1], 2)
    left = add(left[:, 0], left[:, 1], 2)
    right = add(right[:, 0], right[:, 1], 1)
    total = jnp.concatenate([left, right], axis=-1)
    for stride, size in reversed(far_digits(tp_count)):
        total = total.reshape((size, -1) + total.shape[1:])
        kept = total[0]
        for j in range(1, size):
            kept = add(kept, total[j], stride * j)
        total = kept
    return total[0]


def reorder(blocks, rank):
    count = blocks.shape[0]
    step = 1
    while step < count:
        pairs = blocks.reshape((count // (2 * step), 2, step) + blocks.shape[1:])
        flipped = jnp.concatenate([pairs[:, 1:], pairs[:, :1]], axis=1)
        blocks = jnp.where((rank // step) % 2 == 1, flipped, pairs).reshape(blocks.shape)
        step *= 2
    return blocks


def attend_kernel(positions_ref, heads_ref, cos_ref, sin_ref, cache_ref, out_ref):
    kv_cols = KV * HD
    group = HEADS // KV
    position = positions_ref[pl.program_id(0)]
    heads = heads_ref[0].astype(jnp.float32)
    turned = heads[: HEADS + KV]
    turned = turned * cos_ref[0] + pltpu.roll(turned, HD // 2, 1) * sin_ref[0]
    queries = turned[:HEADS]
    new_key = turned[HEADS:].astype(jnp.bfloat16).astype(jnp.float32)
    new_value = heads[HEADS + KV :]
    flat_key = jnp.concatenate([new_key[i : i + 1] for i in range(KV)], axis=1)
    flat_value = jnp.concatenate([new_value[i : i + 1] for i in range(KV)], axis=1)
    own_block = (
        lax.broadcasted_iota(jnp.int32, (HEADS, kv_cols), 0) // group
        == lax.broadcasted_iota(jnp.int32, (HEADS, kv_cols), 1) // HD
    )
    spread = jnp.where(own_block, jnp.concatenate([queries] * KV, axis=1), 0.0).astype(jnp.bfloat16)
    inv_root = HD ** (-0.5)
    cached = (
        lax.dot_general(
            spread,
            cache_ref[0, :, :kv_cols],
            (((1,), (1,)), ((), ())),
            preferred_element_type=jnp.float32,
        )
        * inv_root
    )
    fresh = jnp.sum(spread.astype(jnp.float32) * flat_key, axis=1, keepdims=True) * inv_root
    in_cache = lax.broadcasted_iota(jnp.int32, cached.shape, 1) < position
    cached = jnp.where(in_cache, cached, -1e30)
    peak = jnp.maximum(jnp.max(cached, axis=1, keepdims=True), fresh)
    weights = jnp.exp(cached - peak)
    fresh_w = jnp.exp(fresh - peak)
    total_sum = jnp.sum(weights, axis=1, keepdims=True) + fresh_w
    probs = (weights / total_sum).astype(jnp.bfloat16)
    fresh_p = (fresh_w / total_sum).astype(jnp.bfloat16).astype(jnp.float32)
    result = lax.dot_general(
        probs,
        cache_ref[0, :, kv_cols:],
        (((1,), (0,)), ((), ())),
        preferred_element_type=jnp.float32,
    )
    result = jnp.where(own_block, result + fresh_p * flat_value, 0.0)
    folded = result[:, :HD]
    for i in range(1, KV):
        folded = folded + result[:, i * HD : (i + 1) * HD]
    out_ref[0] = folded.astype(jnp.bfloat16)


def rotation_tables(positions):
    half_dim = HD // 2
    frequency = ROPE_BASE ** (-jnp.arange(half_dim, dtype=jnp.float32) * 2.0 / HD)
    angles = positions.astype(jnp.float32)[:, None] * frequency[None, :]
    cos, sin = jnp.cos(angles), jnp.sin(angles)
    return (
        jnp.concatenate([cos, cos], axis=-1)[:, None, :],
        jnp.concatenate([-sin, sin], axis=-1)[:, None, :],
    )


def attend(projected, cache_rows, positions):
    row_count, cache_len, cache_cols = cache_rows.shape
    head_count = HEADS + 2 * KV
    cos, sin = rotation_tables(positions)
    heads = projected.reshape(row_count, head_count, HD)
    result = pl.pallas_call(
        attend_kernel,
        grid_spec=pltpu.PrefetchScalarGridSpec(
            num_scalar_prefetch=1,
            grid=(row_count,),
            in_specs=[
                pl.BlockSpec((1, head_count, HD), lambda r, pos: (r, 0, 0)),
                pl.BlockSpec((1, 1, HD), lambda r, pos: (r, 0, 0)),
                pl.BlockSpec((1, 1, HD), lambda r, pos: (r, 0, 0)),
                pl.BlockSpec((1, cache_len, cache_cols), lambda r, pos: (r, 0, 0)),
            ],
            out_specs=pl.BlockSpec((1, HEADS, HD), lambda r, pos: (r, 0, 0)),
        ),
        out_shape=jax.ShapeDtypeStruct((row_count, HEADS, HD), jnp.bfloat16),
    )(positions, heads, cos, sin, cache_rows)
    return result.reshape(row_count, HEADS * HD)


def body(
    stream_in,
    kv_cache,
    lengths,
    targets,
    norm_gains,
    w_qkv,
    w_out,
    w_gate_up,
    w_down,
    lm_head,
    fast_in,
    fast_hidden,
    fast_out,
):
    tp_count = lax.axis_size("tp")
    tp_rank = lax.axis_index("tp")
    mem_dev = fast_in.shape[0]
    batch_rows = lengths.shape[0]
    own_rows = stream_in.shape[0]
    all_rows = own_rows * tp_count
    width = stream_in.shape[1]
    first_row = tp_rank * own_rows
    positions = lax.dynamic_slice_in_dim(lengths, first_row % batch_rows, own_rows, 0)
    own_member = first_row // batch_rows
    own_scale = lax.dynamic_index_in_dim(fast_out, own_member, 0, keepdims=True)
    own_normed = rms_norm(stream_in.astype(jnp.float32), norm_gains[0]).astype(jnp.bfloat16)
    attn_in = gather_rows(own_normed, tp_count)
    projected = jnp.dot(attn_in, w_qkv, preferred_element_type=jnp.float32).astype(jnp.bfloat16)
    projected = reorder(projected.reshape(tp_count, own_rows, -1), tp_rank).reshape(projected.shape)
    row_major = lax.all_to_all(projected, "tp", split_axis=0, concat_axis=1, tiled=True)
    attended = attend(row_major, kv_cache, positions)
    head_major = lax.all_to_all(attended, "tp", split_axis=1, concat_axis=0, tiled=True)
    picked = reorder(head_major.reshape(tp_count, own_rows, -1), tp_rank).reshape(head_major.shape)
    attn_sum = scatter_rows(jnp.dot(picked, w_out, preferred_element_type=jnp.float32), tp_count)
    middle = (stream_in.astype(jnp.float32) + attn_sum).astype(jnp.bfloat16)
    own_ffn = rms_norm(middle.astype(jnp.float32), norm_gains[1]).astype(jnp.bfloat16)
    ffn_in = gather_rows(own_ffn, tp_count)
    fast_in = reorder(fast_in, own_member)
    fast_hidden = reorder(fast_hidden, own_member)
    grouped = ffn_in.astype(jnp.float32).reshape(mem_dev, batch_rows, width)
    gate_in = (grouped * fast_in[:, 0][:, None, :]).astype(jnp.bfloat16).reshape(all_rows, width)
    up_in = (grouped * fast_in[:, 1][:, None, :]).astype(jnp.bfloat16).reshape(all_rows, width)
    hidden_cols = w_gate_up.shape[2]
    gate_act = (
        jnp.dot(gate_in, w_gate_up[0], preferred_element_type=jnp.float32).reshape(
            mem_dev, batch_rows, hidden_cols
        )
        * fast_hidden[:, 0][:, None, :]
    )
    up_act = (
        jnp.dot(up_in, w_gate_up[1], preferred_element_type=jnp.float32).reshape(
            mem_dev, batch_rows, hidden_cols
        )
        * fast_hidden[:, 1][:, None, :]
    )
    hidden = (
        (jax.nn.silu(gate_act) * up_act * fast_hidden[:, 2][:, None, :])
        .astype(jnp.bfloat16)
        .reshape(all_rows, hidden_cols)
    )
    picked = hidden
    down_sum = scatter_rows(jnp.dot(picked, w_down, preferred_element_type=jnp.float32), tp_count)
    layer_out = (middle.astype(jnp.float32) + down_sum * own_scale).astype(jnp.bfloat16)
    own_final = rms_norm(layer_out.astype(jnp.float32), norm_gains[2]).astype(jnp.bfloat16)
    cores = lax.axis_size("member")
    core = lax.axis_index("member")
    piece = width // cores
    member_count = mem_dev * cores
    mine = jnp.zeros((own_rows, piece), jnp.float32)
    for step in range(cores):
        target = (core + step) % cores
        part = lax.dynamic_slice_in_dim(own_final, target * piece, piece, 1)
        if step:
            part = lax.ppermute(part, "member", [(i, (i + step) % cores) for i in range(cores)])
        mine = mine + part.astype(jnp.float32)
    far = gather_far(mine.astype(jnp.bfloat16), tp_count)
    far = far.reshape((mem_dev, -1) + far.shape[1:]).astype(jnp.float32)
    summed = jnp.sum(far, axis=0).astype(jnp.bfloat16)
    summed = gather_near(summed, tp_count).reshape(tp_count // mem_dev, own_rows, piece)
    summed = reorder(summed, tp_rank).reshape(batch_rows, piece)
    final_sum = jnp.zeros((batch_rows, width), jnp.bfloat16)
    for step in range(cores):
        part = summed
        if step:
            part = lax.ppermute(summed, "member", [(i, (i + step) % cores) for i in range(cores)])
        source = (core - step) % cores
        final_sum = lax.dynamic_update_slice_in_dim(final_sum, part, source * piece, 1)
    vocab_cols = lm_head.shape[1]
    mean_logit = jnp.dot(final_sum, lm_head, preferred_element_type=jnp.float32) / member_count
    column_ids = tp_rank * vocab_cols + jnp.arange(vocab_cols)
    target_part = jnp.sum(
        jnp.where(column_ids[None, :] == targets[:, None], mean_logit, 0.0), axis=-1
    )
    peak = jnp.max(mean_logit, axis=-1)
    exp_total = jnp.sum(jnp.exp(mean_logit - peak[:, None]), axis=-1)
    stats = jnp.stack([peak, exp_total, target_part])
    mask = 1
    while mask < tp_count:
        other = swap_with(stats, tp_count, mask)
        peak = jnp.maximum(stats[0], other[0])
        total = stats[1] * jnp.exp(stats[0] - peak) + other[1] * jnp.exp(other[0] - peak)
        stats = jnp.stack([peak, total, stats[2] + other[2]])
        mask *= 2
    peak, exp_total, target_logit = stats[0], stats[1], stats[2]
    token_logprob = target_logit - (peak + jnp.log(exp_total))
    return (mean_logit.astype(jnp.bfloat16), token_logprob)


def solution(mesh):
    in_specs = (
        P(("member", "tp"), None),
        P(("member", "tp"), None, None),
        P(),
        P(),
        P(),
        P(None, "tp"),
        P("tp", None),
        P(None, None, "tp"),
        P("tp", None),
        P(None, "tp"),
        P("member", None, None),
        P("member", None, "tp"),
        P("member", None),
    )
    out_specs = (P(None, "tp"), P())
    return jax.shard_map(body, mesh=mesh, in_specs=in_specs, out_specs=out_specs, check_vma=False)
```
